256 devices in a mesh: seq: 64 (over x, z, core), head: 4 (over y).
Axes of the slice: x: 4, y: 4, z: 8, core: 2. Of those that a mesh axis runs over, the one named last changes fastest.
Arguments:
- query: bfloat16 [16384, 4096], P('seq', 'head'), may hold values from -6 to 6
- key: bfloat16 [16384, 4096], P('seq', 'head'), may hold values from -6 to 6
- value: bfloat16 [16384, 4096], P('seq', 'head'), may hold values from -18.75 to 18.75, as said below
- grad_out: bfloat16 [16384, 4096], P('seq', 'head'), may hold values from -6 to 6
- tan_query: bfloat16 [16384, 4096], P('seq', 'head'), may hold values from -6 to 6
- tan_key: bfloat16 [16384, 4096], P('seq', 'head'), may hold values from -6 to 6
- tan_value: bfloat16 [16384, 4096], P('seq', 'head'), may hold values from -6 to 6
- norm_gain: float32 [4096], P('head'), may hold values from 0.25 to 1.75
- prior_state: float32 [32, 128, 128], P('head'), may hold values from -96 to 96
Outputs:
- grad_query: bfloat16 [16384, 4096], P('seq', 'head')
- grad_key: bfloat16 [16384, 4096], P('seq', 'head')
- grad_value: bfloat16 [16384, 4096], P('seq', 'head')
- tan_out: bfloat16 [16384, 4096], P('seq', 'head')
- grad_state: float32 [32, 128, 128], P('head')
The draws below stay inside these ranges and needn't reach their ends.
Inputs may be any that keep to these rules, and one draw needn't show every extreme that they name: `value`: entries bounded in magnitude.
All inputs are finite; a program needn't handle non-finite values.
Results may differ from the reference program's by a relative error of at most 0.0058.
Values sent between devices are 32-bit elements; how exact they have to be, the bound alone decides.
A program may use at most 192 MiB of HBM per device.

```python
import jax
import jax.numpy as jnp
from jax import lax

H = 32
DH = 128
GROUP = 256
TOK_DEV = 256
TOKENS = 16384


def draw_value(key, part):
    first, second = jax.random.split(key)
    heads = jnp.arange(H * DH) // DH
    rise = 3.0 ** (heads.astype(jnp.float32) / (H - 1))
    jitter = jax.random.uniform(second, (H,), jnp.float32, 0.8, 1.25)[heads]
    base = jnp.clip(jax.random.normal(first, (TOKENS, H * DH), jnp.float32), -5.0, 5.0)
    return (base * (rise * jitter)[None, :]).astype(jnp.bfloat16)


def levels(own_key, dims, pieces, smallest, top_value):
    def one(axis_at, blocks):
        draws = jax.random.uniform(jax.random.fold_in(jax.random.fold_in(own_key, 6), axis_at), (blocks,), jnp.float32, smallest / len(pieces), top_value / len(pieces))
        return jnp.repeat(jnp.exp(draws), dims[axis_at] // blocks).reshape((-1,) + (1,) * (len(dims) - axis_at - 1))

    loudness = one(*pieces[0])
    for cut in pieces[1:]:
        loudness = loudness * one(*cut)
    return loudness


def noise(rng, extent, scale, bound, shards=(), held_as=jnp.bfloat16):
    values = jax.random.normal(rng, extent, jnp.float32) * scale
    if len(shards) > 0:
        values = levels(rng, extent, shards, -0.22, 0.18) * values
    return jnp.clip(values, min=-bound, max=bound).astype(held_as)


def setup_inputs(seed: int = 0) -> dict:
    key_list = jax.random.split(jax.random.key(seed), 10)
    query = noise(key_list[0], (TOKENS, H * DH), 1.0, 6.0, ((0, 64), (1, 4)))
    key = noise(key_list[1], (TOKENS, H * DH), 1.0, 6.0, ((0, 64), (1, 4)))
    value = draw_value(jax.random.fold_in(key_list[9], 71), 0)
    grad_out = noise(key_list[3], (TOKENS, H * DH), 1.0, 6.0, ((0, 64), (1, 4)))
    tan_query = noise(key_list[4], (TOKENS, H * DH), 1.0, 6.0, ((0, 64), (1, 4)))
    tan_key = noise(key_list[5], (TOKENS, H * DH), 1.0, 6.0, ((0, 64), (1, 4)))
    tan_value = noise(key_list[6], (TOKENS, H * DH), 1.0, 6.0, ((0, 64), (1, 4)))
    norm_gain = jnp.clip(1.0 + 0.15 * jax.random.normal(key_list[7], (H * DH,), jnp.float32), 0.25, 1.75)
    prior_state = noise(key_list[8], (H, DH, DH), (TOK_DEV ** 0.5), 96.0, ((0, 4),), jnp.float32)
    return dict(query=query, key=key, value=value, grad_out=grad_out, tan_query=tan_query, tan_key=tan_key, tan_value=tan_value, norm_gain=norm_gain, prior_state=prior_state)


eps = 1e-05

def grouped(array):
    return array.reshape(TOKENS // GROUP, GROUP, H, DH)

def pair_sum(left, right):
    return jnp.einsum('shd,she->hde', left.astype(jnp.float32), right.astype(jnp.float32))

def block_mask():
    return jnp.arange(GROUP)[:, None] >= jnp.arange(GROUP)[None, :]

def masked_scores(left, right):
    scores = jnp.einsum('thd,shd->hts', left.astype(jnp.float32), right.astype(jnp.float32))
    return jnp.where(block_mask()[None], scores, 0.0)

def mix_values(weights, values):
    return jnp.einsum('hts,she->the', weights.astype(jnp.float32), values.astype(jnp.float32))

def apply_carried_state(rows, state):
    return jnp.einsum('thd,hde->the', rows.astype(jnp.float32), state.astype(jnp.float32))

def reference(query, key, value, grad_out, tan_query, tan_key, tan_value, norm_gain, prior_state):
    query_full, key_full, value_full = (grouped(query), grouped(key), grouped(value))
    tangent_query_full, tangent_key_full, tangent_value_full = (grouped(tan_query), grouped(tan_key), grouped(tan_value))

    def block_states(items):
        k_blk, v_blk, tk_blk, tv_blk = items
        return (pair_sum(k_blk, v_blk), pair_sum(tk_blk, v_blk) + pair_sum(k_blk, tv_blk))
    kv_sums, tangent_key_value_sums = lax.map(block_states, (key_full, value_full, tangent_key_full, tangent_value_full))
    state = prior_state[None] + jnp.cumsum(kv_sums, 0) - kv_sums
    tangent_state = jnp.cumsum(tangent_key_value_sums, 0) - tangent_key_value_sums
    block_state_entry = state.astype(jnp.bfloat16)
    tangent_block_state = tangent_state.astype(jnp.bfloat16)

    def block_forward_step(items):
        q_blk, k_blk, v_blk, tq_blk, tk_blk, tv_blk, s_blk, ts_blk = items
        a_b = masked_scores(q_blk, k_blk).astype(jnp.bfloat16)
        ta_b = (masked_scores(tq_blk, k_blk) + masked_scores(q_blk, tk_blk)).astype(jnp.bfloat16)
        out_blk = mix_values(a_b, v_blk) + apply_carried_state(q_blk, s_blk)
        tout_blk = mix_values(ta_b, v_blk) + mix_values(a_b, tv_blk) + apply_carried_state(tq_blk, s_blk) + apply_carried_state(q_blk, ts_blk)
        return (out_blk, tout_blk)
    output_full, tangent_output_full = lax.map(block_forward_step, (query_full, key_full, value_full, tangent_query_full, tangent_key_full, tangent_value_full, block_state_entry, tangent_block_state))
    feats = H * DH
    out_flat = output_full.reshape(TOKENS, feats)
    tout_flat = tangent_output_full.reshape(TOKENS, feats)
    gain_grad = norm_gain[None] * grad_out.astype(jnp.float32)
    radius = jnp.sqrt(lax.optimization_barrier(jnp.sum(out_flat * out_flat, 1)) / feats + eps)
    normed = out_flat / radius[:, None]
    tan_coef = lax.optimization_barrier(jnp.sum(out_flat * tout_flat, 1)) / (feats * radius)
    back_coef = lax.optimization_barrier(jnp.sum(out_flat * gain_grad, 1)) / (feats * radius)
    tan_out = (norm_gain[None] * (tout_flat - normed * tan_coef[:, None]) / radius[:, None]).astype(jnp.bfloat16)
    do_all = grouped(((gain_grad - normed * back_coef[:, None]) / radius[:, None]).astype(jnp.bfloat16))

    def grad_block(items):
        q_blk, do_blk = items
        return pair_sum(q_blk, do_blk)
    qdo_sums = lax.map(grad_block, (query_full, do_all))
    grad_state = lax.optimization_barrier(jnp.sum(qdo_sums, 0))
    later_b = (grad_state[None] - jnp.cumsum(qdo_sums, 0)).astype(jnp.bfloat16)

    def backward_block(items):
        q_blk, k_blk, v_blk, do_blk, s_blk, l_blk = items
        a_b = masked_scores(q_blk, k_blk).astype(jnp.bfloat16)
        da_b = masked_scores(do_blk, v_blk).astype(jnp.bfloat16)
        f32 = jnp.float32
        dq_blk = jnp.einsum('hts,shd->thd', da_b.astype(f32), k_blk.astype(f32)) + jnp.einsum('the,hde->thd', do_blk.astype(f32), s_blk.astype(f32))
        dk_blk = jnp.einsum('hts,thd->shd', da_b.astype(f32), q_blk.astype(f32)) + jnp.einsum('she,hde->shd', v_blk.astype(f32), l_blk.astype(f32))
        dv_blk = jnp.einsum('hts,the->she', a_b.astype(f32), do_blk.astype(f32)) + jnp.einsum('shd,hde->she', k_blk.astype(f32), l_blk.astype(f32))
        return (dq_blk.astype(jnp.bfloat16), dk_blk.astype(jnp.bfloat16), dv_blk.astype(jnp.bfloat16))
    dq_all, dk_all, dv_all = lax.map(backward_block, (query_full, key_full, value_full, do_all, block_state_entry, later_b))
    return (dq_all.reshape(TOKENS, feats), dk_all.reshape(TOKENS, feats), dv_all.reshape(TOKENS, feats), tan_out, grad_state)
```

```python
import functools

import jax
import jax.numpy as jnp
from jax import lax
from jax.experimental import pallas as pl
from jax.experimental.pallas import tpu as pltpu
from jax.sharding import PartitionSpec as P

DH = 128
Z, C = 8, 2
NP = 2
KV, TKV, QDO = 0, 1, 2
eps = 1e-05
MESH = pl.DeviceIdType.MESH
f32, bf16 = jnp.float32, jnp.bfloat16


def nn(a, b):
    return lax.dot_general(a, b, (((1,), (0,)), ((), ())), preferred_element_type=f32)


def nt(a, b):
    return lax.dot_general(a, b, (((1,), (1,)), ((), ())), preferred_element_type=f32)


def tn(a, b):
    return lax.dot_general(a, b, (((0,), (0,)), ((), ())), preferred_element_type=f32)


def kernel(
    X,
    Y,
    feats,
    q_in, k_in, v_in, go_in, tq_in, tk_in, tv_in, gain_in, prior_in,
    dq_out, dk_out, dv_out, tan_out, gs_out,
    q, k, v, go, tq, tk, tv, gain, prior, in_sem,
    val, valx, chip, up_rx, x_rx, dn_tx, full, g_tx, g_full,
    core_s, core_r, up_s, up_r, x_s, x_r, dn_s, dn_r, rel_s, rel_r, g_s, g_r, gr_s, gr_r,
    st, st_s, st_r,
    at, o, to, dkl, dvl, do, state, tstate, later, acc_a, acc_b, nrm,
):
    rows, width = q.shape
    heads = width // DH
    half = heads // C
    PR = half * DH // NP
    R = PR // Z

    seq = lax.axis_index("seq")
    y = lax.axis_index("head")
    c = lax.rem(seq, C)
    chip_at = seq // C
    z = lax.rem(chip_at, Z)
    x = chip_at // Z
    mine = c * (half * DH)
    other = (1 - c) * (half * DH)

    def aligned(at_, n):
        return pl.multiple_of(at_, n)

    def seq_dev(x_, z_, c_):
        return {"seq": (x_ * Z + z_) * C + c_}

    sibling = seq_dev(x, z, 1 - c)

    def remote(src, dst, s, r, dev):
        return pltpu.make_async_remote_copy(
            src_ref=src, dst_ref=dst, send_sem=s, recv_sem=r, device_id=dev, device_id_type=MESH
        )

    pairs = [(k_in, k), (v_in, v), (tk_in, tk), (tv_in, tv), (q_in, q), (tq_in, tq), (go_in, go), (gain_in, gain)]
    loads = [pltpu.make_async_copy(s, d, in_sem.at[i]) for i, (s, d) in enumerate(pairs)]
    for load in loads:
        load.start()
    prior_loads = [
        pltpu.make_async_copy(
            prior_in.at[pl.ds(aligned(mine + p * PR + z * R, R), R)], prior.at[p], in_sem.at[len(pairs) + p]
        )
        for p in range(NP)
    ]
    for load in prior_loads:
        load.start()

    barrier = pltpu.get_barrier_semaphore()
    pl.semaphore_signal(barrier, inc=1, device_id=sibling, device_id_type=MESH)

    @pl.loop(1, Z)
    def _(n):
        pl.semaphore_signal(barrier, inc=1, device_id=seq_dev(x, lax.rem(z + n, Z), c), device_id_type=MESH)

    @pl.loop(1, X)
    def _(n):
        pl.semaphore_signal(barrier, inc=1, device_id=seq_dev(lax.rem(x + n, X), z, c), device_id_type=MESH)

    for n in range(1, Y):
        pl.semaphore_signal(barrier, inc=1, device_id={"head": lax.rem(y + n, Y)}, device_id_type=MESH)

    def core_copy(i, p):
        if p < NP:
            part = pl.ds(aligned(other + p * PR, PR), PR)
        else:
            part = pl.ds(aligned(mine, half * DH), half * DH)
        return remote(val.at[i, part], valx.at[i, part], core_s.at[i, p], core_r.at[i, p], sibling)

    def up_copy(i, p, zt, slot):
        src = chip.at[i, pl.ds(aligned(p * PR + zt * R, R), R)]
        return remote(src, up_rx.at[i, p, slot], up_s.at[i, p, zt], up_r.at[i, p, slot], seq_dev(x, zt, c))

    def x_copy(i, p, xt, slot):
        return remote(
            x_rx.at[i, p, x], x_rx.at[i, p, slot], x_s.at[i, p, xt], x_r.at[i, p, slot], seq_dev(xt, z, c)
        )

    def dn_copy(i, p, zt, slot):
        dst = full.at[i, pl.ds(aligned(mine + p * PR + slot * R, R), R)]
        return remote(dn_tx.at[i, p, zt], dst, dn_s.at[i, p, zt], dn_r.at[i, p, slot], seq_dev(x, zt, c))

    def rel_copy(i, p):
        part = pl.ds(aligned(mine + p * PR, PR), PR)
        return remote(full.at[i, part], full.at[i, part], rel_s.at[i, p], rel_r.at[i, p], sibling)

    def g_copy(p, zt, slot):
        dst = g_full.at[pl.ds(aligned(mine + p * PR + slot * R, R), R)]
        return remote(g_tx.at[p], dst, g_s.at[p, zt], g_r.at[p, slot], seq_dev(x, zt, c))

    def gr_copy():
        part = pl.ds(aligned(mine, half * DH), half * DH)
        return remote(g_full.at[part], g_full.at[part], gr_s.at[0], gr_r.at[0], sibling)

    def each_z(body):
        @pl.loop(0, Z - 1)
        def _(j):
            n = lax.rem(j + Z // 2 - 1, Z - 1) + 1
            body(lax.rem(z + n, Z))

    def each_x(body):
        @pl.loop(1, X)
        def _(n):
            body(lax.rem(x + n, X))

    def send_core(i, p):
        core_copy(i, p).start()

    def send_up(i, p):
        core_copy(i, p).wait_recv()
        part = pl.ds(aligned(mine + p * PR, PR), PR)
        chip[i, p * PR : (p + 1) * PR] = val[i, part] + valx[i, part]
        each_z(lambda zt: up_copy(i, p, zt, z).start())
        up_rx[i, p, z] = chip[i, pl.ds(aligned(p * PR + z * R, R), R)]

    def send_x(i, p):
        each_z(lambda zs: up_copy(i, p, zs, zs).wait_recv())
        total = up_rx[i, p, 0]
        for n in range(1, Z):
            total = total + up_rx[i, p, n]
        x_rx[i, p, x] = total
        each_x(lambda xt: x_copy(i, p, xt, x).start())

    def send_down(i, p):
        each_x(lambda xs: x_copy(i, p, xs, xs).wait_recv())
        run = prior[p] if i == KV else jnp.zeros((R, DH), f32)
        for n in range(X):
            reached = (x < n) if i == QDO else (x > n)
            run = run + jnp.where(reached, x_rx[i, p, n], 0.0)
        for n in range(Z - 1, -1, -1) if i == QDO else range(Z):
            dn_tx[i, p, n] = run
            run = run + up_rx[i, p, n]
        each_z(lambda zt: dn_copy(i, p, zt, z).start())
        full[i, pl.ds(aligned(mine + p * PR + z * R, R), R)] = dn_tx[i, p, z]

    def send_total(p):
        total = x_rx[QDO, p, 0]
        for n in range(1, X):
            total = total + x_rx[QDO, p, n]
        g_tx[p] = total
        each_z(lambda zt: g_copy(p, zt, z).start())
        g_full[pl.ds(aligned(mine + p * PR + z * R, R), R)] = g_tx[p]

    def relay(i, p):
        each_z(lambda zs: dn_copy(i, p, zs, zs).wait_recv())
        rel_copy(i, p).start()

    def finish(i):
        core_copy(i, NP).wait_recv()
        for p in range(NP):
            rel_copy(i, p).wait_recv()

    def entering(i, h):
        part = slice(h * DH, (h + 1) * DH)
        own_chip = (c == 0) if i == QDO else (c == 1)
        return (full[i, part] + jnp.where(own_chip, valx[i, part], 0.0)).astype(bf16)

    def cols(h):
        return pl.ds(aligned(h * DH, DH), DH)

    def head_rows(h):
        return pl.ds(aligned(h * DH, DH), DH)

    def key_value(h):
        val[KV, head_rows(h)] = tn(k[:, cols(h)], v[:, cols(h)])

    def tangent_key_value(h):
        val[TKV, head_rows(h)] = tn(tk[:, cols(h)], v[:, cols(h)]) + tn(k[:, cols(h)], tv[:, cols(h)])

    def over(first, count, body):
        for j in range(count):
            body(first + j)

    up_mask = lax.broadcasted_iota(jnp.int32, (rows, rows), 0) <= lax.broadcasted_iota(jnp.int32, (rows, rows), 1)
    low_mask = lax.broadcasted_iota(jnp.int32, (rows, rows), 0) >= lax.broadcasted_iota(jnp.int32, (rows, rows), 1)

    def masked(scores, mask):
        return jnp.where(mask, scores, 0.0).astype(bf16)

    def block_forward(lo, hi):
        @pl.loop(lo, hi)
        def _(h):
            qh, kh, vh = q[:, cols(h)], k[:, cols(h)], v[:, cols(h)]
            tqh, tkh, tvh = tq[:, cols(h)], tk[:, cols(h)], tv[:, cols(h)]
            a = masked(nt(qh, kh), low_mask)
            ta = masked(nt(tqh, kh) + nt(qh, tkh), low_mask)
            at[h] = masked(nt(kh, qh), up_mask)
            o[:, cols(h)] = nn(a, vh)
            to[:, cols(h)] = nn(ta, vh) + nn(a, tvh)

    def block_backward(lo, hi):
        @pl.loop(lo, hi)
        def _(h):
            qh, kh, vh, doh = q[:, cols(h)], k[:, cols(h)], v[:, cols(h)], do[:, cols(h)]
            da = masked(nt(doh, vh), low_mask)
            dat = masked(nt(vh, doh), up_mask)
            dq_out[:, cols(h)] = (nn(da, kh) + nt(doh, state[head_rows(h)])).astype(bf16)
            dkl[:, cols(h)] = nn(dat, qh)
            dvl[:, cols(h)] = nn(at[h], doh)

    def lane_sums(acc):
        return jnp.sum(acc[...].T, axis=0, keepdims=True)

    def spread(row):
        return jnp.broadcast_to(row, (DH, rows)).T

    def st_copy(i, yt, slot):
        return remote(st.at[i, y], st.at[i, slot], st_s.at[i, yt], st_r.at[i, slot], {"head": yt})

    def exchange(i, accs):
        st[i, y] = jnp.concatenate([lane_sums(a) for a in accs] + [jnp.zeros((8 - len(accs), rows), f32)], axis=0)
        for n in range(1, Y):
            st_copy(i, lax.rem(y + n, Y), y).start()

    def exchanged(i):
        for n in range(1, Y):
            ys = lax.rem(y + n, Y)
            st_copy(i, ys, ys).wait_recv()
        total = st[i, 0]
        for n in range(1, Y):
            total = total + st[i, n]
        return total

    loads[0].wait()
    loads[1].wait()
    over((1 - c) * half, half, key_value)
    pl.semaphore_wait(barrier, (C - 1) + (Z - 1) + (X - 1) + (Y - 1))
    for p in range(NP):
        send_core(KV, p)
    over(c * half, half, key_value)
    send_core(KV, NP)
    loads[2].wait()
    loads[3].wait()
    over((1 - c) * half, half, tangent_key_value)
    for p in range(NP):
        send_up(KV, p)
    for p in range(NP):
        send_core(TKV, p)
    over(c * half, half, tangent_key_value)
    send_core(TKV, NP)
    for p in range(NP):
        send_up(TKV, p)
    for load in loads[4:]:
        load.wait()
    for load in prior_loads:
        load.wait()
    block_forward(0, 3)
    send_x(KV, 0)
    send_x(KV, 1)
    block_forward(3, 5)
    send_down(KV, 0)
    send_down(KV, 1)
    send_x(TKV, 0)
    send_x(TKV, 1)
    block_forward(5, heads)
    relay(KV, 0)
    relay(KV, 1)
    send_down(TKV, 0)
    send_down(TKV, 1)
    finish(KV)
    acc_a[...] = jnp.zeros((rows, DH), f32)
    acc_b[...] = jnp.zeros((rows, DH), f32)
    for h in range(heads):
        part = slice(h * DH, (h + 1) * DH)
        state[part] = entering(KV, h)
        out = o[:, part] + nn(q[:, part], state[part])
        o[:, part] = out
        acc_a[...] += out * out
        acc_b[...] += out * (gain[h : h + 1] * go[:, part].astype(f32))
    exchange(0, [acc_a, acc_b])
    relay(TKV, 0)
    relay(TKV, 1)

    sums = exchanged(0)
    inv = 1.0 / jnp.sqrt(sums[0:1] / feats + eps)
    inv2 = inv * inv
    nrm[...] = spread(inv)
    back = spread(sums[1:2] / feats * inv * inv2)

    def cotangent(h):
        g = gain[pl.ds(h, 1)] * go[:, cols(h)].astype(f32)
        doh = (g * nrm[...] - o[:, cols(h)] * back).astype(bf16)
        do[:, cols(h)] = doh
        val[QDO, head_rows(h)] = tn(q[:, cols(h)], doh)

    over((1 - c) * half, half, cotangent)
    for p in range(NP):
        send_core(QDO, p)
    over(c * half, half, cotangent)
    send_core(QDO, NP)
    block_backward(0, 2)
    for p in range(NP):
        send_up(QDO, p)
    finish(TKV)
    acc_a[...] = jnp.zeros((rows, DH), f32)
    for h in range(heads):
        part = slice(h * DH, (h + 1) * DH)
        tout = to[:, part] + nn(tq[:, part], state[part]) + nn(q[:, part], entering(TKV, h))
        to[:, part] = tout
        acc_a[...] += o[:, part] * tout
    exchange(1, [acc_a])
    block_backward(2, 5)
    send_x(QDO, 0)
    send_x(QDO, 1)
    block_backward(5, heads)
    send_down(QDO, 0)
    send_down(QDO, 1)
    send_total(0)
    send_total(1)
    tangent = spread(exchanged(1)[0:1] / feats * inv * inv2)
    for h in range(heads):
        part = slice(h * DH, (h + 1) * DH)
        tan_out[:, part] = (gain[h : h + 1] * (to[:, part] * nrm[...] - o[:, part] * tangent)).astype(bf16)
    relay(QDO, 0)
    relay(QDO, 1)
    finish(QDO)
    for h in range(heads):
        part = slice(h * DH, (h + 1) * DH)
        after = entering(QDO, h)
        dk_out[:, part] = (dkl[:, part] + nt(v[:, part], after)).astype(bf16)
        dv_out[:, part] = (dvl[:, part] + nn(k[:, part], after)).astype(bf16)
    for p in range(NP):
        each_z(lambda zs: g_copy(p, zs, zs).wait_recv())
    gr_copy().start()
    gr_copy().wait_recv()
    gs_out[...] = g_full[...]

    for i in range(3):
        for p in range(NP + 1):
            core_copy(i, p).wait_send()
        for p in range(NP):
            each_z(lambda zt: up_copy(i, p, zt, z).wait_send())
            each_x(lambda xt: x_copy(i, p, xt, x).wait_send())
            each_z(lambda zt: dn_copy(i, p, zt, z).wait_send())
            rel_copy(i, p).wait_send()
    for p in range(NP):
        each_z(lambda zt: g_copy(p, zt, z).wait_send())
    gr_copy().wait_send()
    for i in range(2):
        for n in range(1, Y):
            st_copy(i, lax.rem(y + n, Y), y).wait_send()


def solution(mesh):
    X = mesh.shape["seq"] // (Z * C)
    Y = mesh.shape["head"]

    def per_device(query, key, value, grad_out, tan_query, tan_key, tan_value, norm_gain, prior_state):
        rows, width = query.shape
        heads = width // DH
        half = heads // C
        PR = half * DH // NP
        R = PR // Z
        vmem = pltpu.VMEM
        dma = pltpu.SemaphoreType.DMA
        wide = jax.ShapeDtypeStruct((rows, width), bf16)
        any_spec = pl.BlockSpec(memory_space=pl.ANY)
        vmem_spec = pl.BlockSpec(memory_space=pltpu.VMEM)
        outs = pl.pallas_call(
            functools.partial(kernel, X, Y, width * Y),
            out_shape=[wide] * 4 + [jax.ShapeDtypeStruct((heads * DH, DH), f32)],
            in_specs=[any_spec] * 9,
            out_specs=[vmem_spec] * 5,
            scratch_shapes=[vmem((rows, width), bf16)] * 7
            + [
                vmem((heads, DH), f32),
                vmem((NP, R, DH), f32),
                dma((8 + NP,)),
                vmem((3, heads * DH, DH), f32),
                vmem((3, heads * DH, DH), f32),
                vmem((3, half * DH, DH), f32),
                vmem((3, NP, Z, R, DH), f32),
                vmem((3, NP, X, R, DH), f32),
                vmem((3, NP, Z, R, DH), f32),
                vmem((3, heads * DH, DH), f32),
                vmem((NP, R, DH), f32),
                vmem((heads * DH, DH), f32),
                dma((3, NP + 1)),
                dma((3, NP + 1)),
                dma((3, NP, Z)),
                dma((3, NP, Z)),
                dma((3, NP, X)),
                dma((3, NP, X)),
                dma((3, NP, Z)),
                dma((3, NP, Z)),
                dma((3, NP)),
                dma((3, NP)),
                dma((NP, Z)),
                dma((NP, Z)),
                dma((1,)),
                dma((1,)),
                vmem((2, Y, 8, rows), f32),
                dma((2, Y)),
                dma((2, Y)),
                vmem((heads, rows, rows), bf16),
                vmem((rows, width), f32),
                vmem((rows, width), f32),
                vmem((rows, width), f32),
                vmem((rows, width), f32),
                vmem((rows, width), bf16),
                vmem((heads * DH, DH), bf16),
                vmem((heads * DH, DH), bf16),
                vmem((heads * DH, DH), bf16),
                vmem((rows, DH), f32),
                vmem((rows, DH), f32),
                vmem((rows, DH), f32),
            ],
            compiler_params=pltpu.CompilerParams(
                collective_id=0, has_side_effects=True, vmem_limit_bytes=60 * 1024 * 1024
            ),
        )(
            query, key, value, grad_out, tan_query, tan_key, tan_value,
            norm_gain.reshape(heads, DH), prior_state.reshape(heads * DH, DH),
        )
        return (*outs[:4], outs[4].reshape(heads, DH, DH))

    wide, per_head = P("seq", "head"), P("head", None, None)
    return jax.shard_map(
        per_device,
        mesh=mesh,
        in_specs=(wide,) * 7 + (P("head"), per_head),
        out_specs=(wide,) * 4 + (per_head,),
        check_vma=False,
    )
```

```python
import functools

import jax
import jax.numpy as jnp
from jax import lax
from jax.experimental import pallas as pl
from jax.experimental.pallas import tpu as pltpu
from jax.sharding import PartitionSpec as P

DH = 128
Z, C = 8, 2
NP = 2
KV, TKV, QDO = 0, 1, 2
eps = 1e-05
MESH = pl.DeviceIdType.MESH
f32, bf16 = jnp.float32, jnp.bfloat16


def nn(a, b):
    return lax.dot_general(a, b, (((1,), (0,)), ((), ())), preferred_element_type=f32)


def nt(a, b):
    return lax.dot_general(a, b, (((1,), (1,)), ((), ())), preferred_element_type=f32)


def tn(a, b):
    return lax.dot_general(a, b, (((0,), (0,)), ((), ())), preferred_element_type=f32)


def kernel(
    X,
    Y,
    feats,
    q_in, k_in, v_in, go_in, tq_in, tk_in, tv_in, gain_in, prior_in,
    dq_hbm, dk_hbm, dv_hbm, tan_hbm, gs_hbm,
    dq_out, dk_out, dv_out, tan_out, gs_out, out_sem,
    q, k, v, go, tq, tk, tv, gain, prior, in_sem,
    val, valx, chip, up_rx, x_rx, dn_tx, full, g_tx, g_all,
    core_s, core_r, up_s, up_r, x_s, x_r, dn_s, dn_r, rel_s, rel_r, g_s, g_r, gx_s, gx_r, gr_s, gr_r,
    st, st_s, st_r,
    at, o, to, dkl, dvl, do, state, tstate, later, acc_a, acc_b, nrm,
):
    rows, width = q.shape
    heads = width // DH
    half = heads // C
    PR = half * DH // NP
    R = PR // Z
    RX = R // X

    seq = lax.axis_index("seq")
    y = lax.axis_index("head")
    c = lax.rem(seq, C)
    chip_at = seq // C
    z = lax.rem(chip_at, Z)
    x = chip_at // Z
    mine = c * (half * DH)
    other = (1 - c) * (half * DH)

    def aligned(at_, n):
        return pl.multiple_of(at_, n)

    def seq_dev(x_, z_, c_):
        return {"seq": (x_ * Z + z_) * C + c_}

    sibling = seq_dev(x, z, 1 - c)

    def remote(src, dst, s, r, dev):
        return pltpu.make_async_remote_copy(
            src_ref=src, dst_ref=dst, send_sem=s, recv_sem=r, device_id=dev, device_id_type=MESH
        )

    pairs = [(k_in, k), (v_in, v), (tk_in, tk), (tv_in, tv), (q_in, q), (tq_in, tq), (go_in, go), (gain_in, gain)]
    loads = [pltpu.make_async_copy(s, d, in_sem.at[i]) for i, (s, d) in enumerate(pairs)]
    for load in loads:
        load.start()
    prior_loads = [
        pltpu.make_async_copy(
            prior_in.at[pl.ds(aligned(mine + p * PR + z * R, R), R)], prior.at[p], in_sem.at[len(pairs) + p]
        )
        for p in range(NP)
    ]
    for load in prior_loads:
        load.start()

    barrier = pltpu.get_barrier_semaphore()
    pl.semaphore_signal(barrier, inc=1, device_id=sibling, device_id_type=MESH)

    @pl.loop(1, Z)
    def _(n):
        pl.semaphore_signal(barrier, inc=1, device_id=seq_dev(x, lax.rem(z + n, Z), c), device_id_type=MESH)

    @pl.loop(1, X)
    def _(n):
        pl.semaphore_signal(barrier, inc=1, device_id=seq_dev(lax.rem(x + n, X), z, c), device_id_type=MESH)

    for n in range(1, Y):
        pl.semaphore_signal(barrier, inc=1, device_id={"head": lax.rem(y + n, Y)}, device_id_type=MESH)

    def core_copy(i, p):
        if p < NP:
            part = pl.ds(aligned(other + p * PR, PR), PR)
        else:
            part = pl.ds(aligned(mine, half * DH), half * DH)
        return remote(val.at[i, part], valx.at[i, part], core_s.at[i, p], core_r.at[i, p], sibling)

    def up_copy(i, p, zt, slot):
        src = chip.at[i, pl.ds(aligned(p * PR + zt * R, R), R)]
        return remote(src, up_rx.at[i, p, slot], up_s.at[i, p, zt], up_r.at[i, p, slot], seq_dev(x, zt, c))

    def x_copy(i, p, xt, slot):
        return remote(
            x_rx.at[i, p, x], x_rx.at[i, p, slot], x_s.at[i, p, xt], x_r.at[i, p, slot], seq_dev(xt, z, c)
        )

    def dn_copy(i, p, zt, slot):
        dst = full.at[i, pl.ds(aligned(mine + p * PR + slot * R, R), R)]
        return remote(dn_tx.at[i, p, zt], dst, dn_s.at[i, p, zt], dn_r.at[i, p, slot], seq_dev(x, zt, c))

    def rel_copy(i, p):
        part = pl.ds(aligned(mine + p * PR, PR), PR)
        return remote(full.at[i, part], full.at[i, part], rel_s.at[i, p], rel_r.at[i, p], sibling)

    def g_copy(p, zt, slot):
        return remote(g_tx.at[p], g_all.at[c, p, x, slot], g_s.at[p, zt], g_r.at[p, slot], seq_dev(x, zt, c))

    def gx_copy(p, xt, slot):
        return remote(
            g_all.at[c, p, x], g_all.at[c, p, slot], gx_s.at[p, xt], gx_r.at[p, slot], seq_dev(xt, z, c)
        )

    def gr_copy():
        return remote(g_all.at[c], g_all.at[c], gr_s.at[0], gr_r.at[0], sibling)

    def each_z(body):
        @pl.loop(0, Z - 1)
        def _(j):
            n = lax.rem(j + Z // 2 - 1, Z - 1) + 1
            body(lax.rem(z + n, Z))

    def each_x(body):
        @pl.loop(1, X)
        def _(n):
            body(lax.rem(x + n, X))

    def send_core(i, p):
        core_copy(i, p).start()

    def send_up(i, p):
        core_copy(i, p).wait_recv()
        part = pl.ds(aligned(mine + p * PR, PR), PR)
        chip[i, p * PR : (p + 1) * PR] = val[i, part] + valx[i, part]
        each_z(lambda zt: up_copy(i, p, zt, z).start())
        up_rx[i, p, z] = chip[i, pl.ds(aligned(p * PR + z * R, R), R)]

    def send_x(i, p):
        each_z(lambda zs: up_copy(i, p, zs, zs).wait_recv())
        total = up_rx[i, p, 0]
        for n in range(1, Z):
            total = total + up_rx[i, p, n]
        x_rx[i, p, x] = total
        each_x(lambda xt: x_copy(i, p, xt, x).start())

    def arrive_x(i, p):
        each_x(lambda xs: x_copy(i, p, xs, xs).wait_recv())

    def send_down(i, p):
        run = prior[p] if i == KV else jnp.zeros((R, DH), f32)
        for n in range(X):
            reached = (x < n) if i == QDO else (x > n)
            run = run + jnp.where(reached, x_rx[i, p, n], 0.0)
        for n in range(Z - 1, -1, -1) if i == QDO else range(Z):
            dn_tx[i, p, n] = run
            run = run + up_rx[i, p, n]
        each_z(lambda zt: dn_copy(i, p, zt, z).start())
        full[i, pl.ds(aligned(mine + p * PR + z * R, R), R)] = dn_tx[i, p, z]

    def send_total(p):
        piece = pl.ds(aligned(x * RX, RX), RX)
        total = x_rx[QDO, p, 0, piece]
        for n in range(1, X):
            total = total + x_rx[QDO, p, n, piece]
        g_tx[p] = total
        each_z(lambda zt: g_copy(p, zt, z).start())
        g_all[c, p, x, z] = total

    def spread_total(p):
        each_z(lambda zs: g_copy(p, zs, zs).wait_recv())
        each_x(lambda xt: gx_copy(p, xt, x).start())

    def relay(i, p):
        each_z(lambda zs: dn_copy(i, p, zs, zs).wait_recv())
        rel_copy(i, p).start()

    def finish(i):
        core_copy(i, NP).wait_recv()
        for p in range(NP):
            rel_copy(i, p).wait_recv()

    def entering(i, h):
        part = slice(h * DH, (h + 1) * DH)
        own_chip = (c == 0) if i == QDO else (c == 1)
        return (full[i, part] + jnp.where(own_chip, valx[i, part], 0.0)).astype(bf16)

    def cols(h):
        return pl.ds(aligned(h * DH, DH), DH)

    def head_rows(h):
        return pl.ds(aligned(h * DH, DH), DH)

    def key_value(h):
        val[KV, head_rows(h)] = tn(k[:, cols(h)], v[:, cols(h)])

    def tangent_key_value(h):
        val[TKV, head_rows(h)] = tn(tk[:, cols(h)], v[:, cols(h)]) + tn(k[:, cols(h)], tv[:, cols(h)])

    def over(first, count, body):
        for j in range(count):
            body(first + j)

    up_mask = lax.broadcasted_iota(jnp.int32, (rows, rows), 0) <= lax.broadcasted_iota(jnp.int32, (rows, rows), 1)
    low_mask = lax.broadcasted_iota(jnp.int32, (rows, rows), 0) >= lax.broadcasted_iota(jnp.int32, (rows, rows), 1)

    def masked(scores, mask):
        return jnp.where(mask, scores, 0.0).astype(bf16)

    def block_forward(lo, hi):
        @pl.loop(lo, hi)
        def _(h):
            qh, kh, vh = q[:, cols(h)], k[:, cols(h)], v[:, cols(h)]
            tqh, tkh, tvh = tq[:, cols(h)], tk[:, cols(h)], tv[:, cols(h)]
            a = masked(nt(qh, kh), low_mask)
            ta = masked(nt(tqh, kh) + nt(qh, tkh), low_mask)
            at[h] = masked(nt(kh, qh), up_mask)
            o[:, cols(h)] = nn(a, vh)
            to[:, cols(h)] = nn(ta, vh) + nn(a, tvh)

    def block_backward(lo, hi):
        @pl.loop(lo, hi)
        def _(h):
            qh, kh, vh, doh = q[:, cols(h)], k[:, cols(h)], v[:, cols(h)], do[:, cols(h)]
            da = masked(nt(doh, vh), low_mask)
            dat = masked(nt(vh, doh), up_mask)
            dq_out[:, cols(h)] = (nn(da, kh) + nt(doh, state[head_rows(h)])).astype(bf16)
            dkl[:, cols(h)] = nn(dat, qh)
            dvl[:, cols(h)] = nn(at[h], doh)

    def lane_sums(acc):
        return jnp.sum(acc[...].T, axis=0, keepdims=True)

    def spread(row):
        return jnp.broadcast_to(row, (DH, rows)).T

    def st_copy(i, yt, slot):
        return remote(st.at[i, y], st.at[i, slot], st_s.at[i, yt], st_r.at[i, slot], {"head": yt})

    def exchange(i, accs):
        st[i, y] = jnp.concatenate([lane_sums(a) for a in accs] + [jnp.zeros((8 - len(accs), rows), f32)], axis=0)
        for n in range(1, Y):
            st_copy(i, lax.rem(y + n, Y), y).start()

    def exchanged(i):
        for n in range(1, Y):
            ys = lax.rem(y + n, Y)
            st_copy(i, ys, ys).wait_recv()
        total = st[i, 0]
        for n in range(1, Y):
            total = total + st[i, n]
        return total

    outs = [(dq_out, dq_hbm), (dk_out, dk_hbm), (dv_out, dv_hbm), (tan_out, tan_hbm), (gs_out, gs_hbm)]
    stores = [pltpu.make_async_copy(s, d, out_sem.at[i]) for i, (s, d) in enumerate(outs)]

    def store_out(i):
        stores[i].start()

    loads[0].wait()
    loads[1].wait()
    over((1 - c) * half, half, key_value)
    pl.semaphore_wait(barrier, (C - 1) + (Z - 1) + (X - 1) + (Y - 1))
    for p in range(NP):
        send_core(KV, p)
    over(c * half, half, key_value)
    send_core(KV, NP)
    loads[2].wait()
    loads[3].wait()
    over((1 - c) * half, half, tangent_key_value)
    for p in range(NP):
        send_up(KV, p)
    for p in range(NP):
        send_core(TKV, p)
    over(c * half, half, tangent_key_value)
    send_core(TKV, NP)
    for p in range(NP):
        send_up(TKV, p)
    for load in loads[4:]:
        load.wait()
    for load in prior_loads:
        load.wait()
    block_forward(0, 3)
    send_x(KV, 0)
    send_x(KV, 1)
    block_forward(3, 5)
    for p in range(NP):
        arrive_x(KV, p)
        send_down(KV, p)
    send_x(TKV, 0)
    send_x(TKV, 1)
    block_forward(5, heads)
    relay(KV, 0)
    relay(KV, 1)
    for p in range(NP):
        arrive_x(TKV, p)
        send_down(TKV, p)
    finish(KV)
    acc_a[...] = jnp.zeros((rows, DH), f32)
    acc_b[...] = jnp.zeros((rows, DH), f32)
    for h in range(heads):
        part = slice(h * DH, (h + 1) * DH)
        state[part] = entering(KV, h)
        out = o[:, part] + nn(q[:, part], state[part])
        o[:, part] = out
        acc_a[...] += out * out
        acc_b[...] += out * (gain[h : h + 1] * go[:, part].astype(f32))
    exchange(0, [acc_a, acc_b])
    relay(TKV, 0)
    relay(TKV, 1)

    sums = exchanged(0)
    inv = 1.0 / jnp.sqrt(sums[0:1] / feats + eps)
    inv2 = inv * inv
    nrm[...] = spread(inv)
    back = spread(sums[1:2] / feats * inv * inv2)

    def cotangent(h):
        g = gain[pl.ds(h, 1)] * go[:, cols(h)].astype(f32)
        doh = (g * nrm[...] - o[:, cols(h)] * back).astype(bf16)
        do[:, cols(h)] = doh
        val[QDO, head_rows(h)] = tn(q[:, cols(h)], doh)

    over((1 - c) * half, half, cotangent)
    for p in range(NP):
        send_core(QDO, p)
    over(c * half, half, cotangent)
    send_core(QDO, NP)
    block_backward(0, 2)
    for p in range(NP):
        send_up(QDO, p)
    finish(TKV)
    acc_a[...] = jnp.zeros((rows, DH), f32)
    for h in range(heads):
        part = slice(h * DH, (h + 1) * DH)
        tout = to[:, part] + nn(tq[:, part], state[part]) + nn(q[:, part], entering(TKV, h))
        to[:, part] = tout
        acc_a[...] += o[:, part] * tout
    exchange(1, [acc_a])
    block_backward(2, 5)
    send_x(QDO, 0)
    send_x(QDO, 1)
    block_backward(5, heads)
    store_out(0)
    for p in range(NP):
        arrive_x(QDO, p)
        send_total(p)
    for p in range(NP):
        send_down(QDO, p)
    tangent = spread(exchanged(1)[0:1] / feats * inv * inv2)
    for h in range(heads):
        part = slice(h * DH, (h + 1) * DH)
        tan_out[:, part] = (gain[h : h + 1] * (to[:, part] * nrm[...] - o[:, part] * tangent)).astype(bf16)
    store_out(3)
    for p in range(NP):
        spread_total(p)
    relay(QDO, 0)
    relay(QDO, 1)
    for p in range(NP):
        each_x(lambda xs: gx_copy(p, xs, xs).wait_recv())
    gr_copy().start()
    finish(QDO)
    for h in range(heads):
        part = slice(h * DH, (h + 1) * DH)
        after = entering(QDO, h)
        dk_out[:, part] = (dkl[:, part] + nt(v[:, part], after)).astype(bf16)
        dv_out[:, part] = (dvl[:, part] + nn(k[:, part], after)).astype(bf16)
    store_out(1)
    store_out(2)
    gr_copy().wait_recv()
    for ch in range(C):
        for p in range(NP):
            for zs in range(Z):
                for xs in range(X):
                    at_ = ch * half * DH + p * PR + zs * R + xs * RX
                    gs_out[at_ : at_ + RX] = g_all[ch, p, xs, zs]
    store_out(4)
    for store in stores:
        store.wait()

    for i in range(3):
        for p in range(NP + 1):
            core_copy(i, p).wait_send()
        for p in range(NP):
            each_z(lambda zt: up_copy(i, p, zt, z).wait_send())
            each_x(lambda xt: x_copy(i, p, xt, x).wait_send())
            each_z(lambda zt: dn_copy(i, p, zt, z).wait_send())
            rel_copy(i, p).wait_send()
    for p in range(NP):
        each_z(lambda zt: g_copy(p, zt, z).wait_send())
        each_x(lambda xt: gx_copy(p, xt, x).wait_send())
    gr_copy().wait_send()
    for i in range(2):
        for n in range(1, Y):
            st_copy(i, lax.rem(y + n, Y), y).wait_send()


def copy_out(*refs):
    n = (len(refs) - 2) // 3
    ins, outs, held, in_sem, out_sem = refs[:n], refs[n : 2 * n], refs[2 * n : 3 * n], refs[-2], refs[-1]
    loads = [pltpu.make_async_copy(ins[i], held[i], in_sem.at[i]) for i in range(n)]
    stores = [pltpu.make_async_copy(held[i], outs[i], out_sem.at[i]) for i in range(n)]
    for load in loads:
        load.start()
    for load, store in zip(loads, stores):
        load.wait()
        store.start()
    for store in stores:
        store.wait()


def solution(mesh):
    X = mesh.shape["seq"] // (Z * C)
    Y = mesh.shape["head"]

    def per_device(query, key, value, grad_out, tan_query, tan_key, tan_value, norm_gain, prior_state):
        rows, width = query.shape
        heads = width // DH
        half = heads // C
        PR = half * DH // NP
        R = PR // Z
        vmem = pltpu.VMEM
        dma = pltpu.SemaphoreType.DMA
        wide = jax.ShapeDtypeStruct((rows, width), bf16)
        any_spec = pl.BlockSpec(memory_space=pl.ANY)
        outs = pl.pallas_call(
            functools.partial(kernel, X, Y, width * Y),
            out_shape=[wide] * 4 + [jax.ShapeDtypeStruct((heads * DH, DH), f32)],
            in_specs=[any_spec] * 9,
            out_specs=[any_spec] * 5,
            scratch_shapes=[vmem((rows, width), bf16)] * 4
            + [vmem((heads * DH, DH), f32), dma((5,))]
            + [vmem((rows, width), bf16)] * 7
            + [
                vmem((heads, DH), f32),
                vmem((NP, R, DH), f32),
                dma((8 + NP,)),
                vmem((3, heads * DH, DH), f32),
                vmem((3, heads * DH, DH), f32),
                vmem((3, half * DH, DH), f32),
                vmem((3, NP, Z, R, DH), f32),
                vmem((3, NP, X, R, DH), f32),
                vmem((3, NP, Z, R, DH), f32),
                vmem((3, heads * DH, DH), f32),
                vmem((NP, R // X, DH), f32),
                vmem((C, NP, X, Z, R // X, DH), f32),
                dma((3, NP + 1)),
                dma((3, NP + 1)),
                dma((3, NP, Z)),
                dma((3, NP, Z)),
                dma((3, NP, X)),
                dma((3, NP, X)),
                dma((3, NP, Z)),
                dma((3, NP, Z)),
                dma((3, NP)),
                dma((3, NP)),
                dma((NP, Z)),
                dma((NP, Z)),
                dma((NP, X)),
                dma((NP, X)),
                dma((1,)),
                dma((1,)),
                vmem((2, Y, 8, rows), f32),
                dma((2, Y)),
                dma((2, Y)),
                vmem((heads, rows, rows), bf16),
                vmem((rows, width), f32),
                vmem((rows, width), f32),
                vmem((rows, width), f32),
                vmem((rows, width), f32),
                vmem((rows, width), bf16),
                vmem((heads * DH, DH), bf16),
                vmem((heads * DH, DH), bf16),
                vmem((heads * DH, DH), bf16),
                vmem((rows, DH), f32),
                vmem((rows, DH), f32),
                vmem((rows, DH), f32),
            ],
            compiler_params=pltpu.CompilerParams(
                collective_id=0, has_side_effects=True, vmem_limit_bytes=60 * 1024 * 1024
            ),
        )(
            query, key, value, grad_out, tan_query, tan_key, tan_value,
            norm_gain.reshape(heads, DH), prior_state.reshape(heads * DH, DH),
        )
        outs = pl.pallas_call(
            copy_out,
            out_shape=[wide] * 4 + [jax.ShapeDtypeStruct((heads * DH, DH), f32)],
            in_specs=[any_spec] * 5,
            out_specs=[any_spec] * 5,
            scratch_shapes=[vmem((rows, width), bf16)] * 4 + [vmem((heads * DH, DH), f32), dma((5,)), dma((5,))],
        )(*outs)
        return (*outs[:4], outs[4].reshape(heads, DH, DH))

    wide, per_head = P("seq", "head"), P("head", None, None)
    return jax.shard_map(
        per_device,
        mesh=mesh,
        in_specs=(wide,) * 7 + (P("head"), per_head),
        out_specs=(wide,) * 4 + (per_head,),
        check_vma=False,
    )
```

```python
import functools

import jax
import jax.numpy as jnp
from jax import lax
from jax.experimental import pallas as pl
from jax.experimental.pallas import tpu as pltpu
from jax.sharding import PartitionSpec as P

DH = 128
Z, C = 8, 2
NP = 2
KV, TKV, QDO = 0, 1, 2
eps = 1e-05
MESH = pl.DeviceIdType.MESH
f32, bf16 = jnp.float32, jnp.bfloat16


def nn(a, b):
    return lax.dot_general(a, b, (((1,), (0,)), ((), ())), preferred_element_type=f32)


def nt(a, b):
    return lax.dot_general(a, b, (((1,), (1,)), ((), ())), preferred_element_type=f32)


def tn(a, b):
    return lax.dot_general(a, b, (((0,), (0,)), ((), ())), preferred_element_type=f32)


def kernel(
    X,
    Y,
    feats,
    q_in, k_in, v_in, go_in, tq_in, tk_in, tv_in, gain_in, prior_in,
    dq_hbm, dk_hbm, dv_hbm, tan_hbm, gs_hbm,
    dq_out, dk_out, dv_out, tan_out, gs_out, out_sem,
    q, k, v, go, tq, tk, tv, gain, prior, in_sem,
    val, valx, chip, up_rx, x_rx, dn_tx, full, g_tx, g_all,
    core_s, core_r, up_s, up_r, x_s, x_r, dn_s, dn_r, rel_s, rel_r, g_s, g_r, gx_s, gx_r, gr_s, gr_r,
    st, st_s, st_r,
    at, o, to, dkl, dvl, do, state, tstate, later, acc_a, acc_b, nrm,
):
    rows, width = q.shape
    heads = width // DH
    half = heads // C
    PR = half * DH // NP
    R = PR // Z
    RX = R // X

    seq = lax.axis_index("seq")
    y = lax.axis_index("head")
    c = lax.rem(seq, C)
    chip_at = seq // C
    z = lax.rem(chip_at, Z)
    x = chip_at // Z
    mine = c * (half * DH)
    other = (1 - c) * (half * DH)

    def aligned(at_, n):
        return pl.multiple_of(at_, n)

    def seq_dev(x_, z_, c_):
        return {"seq": (x_ * Z + z_) * C + c_}

    sibling = seq_dev(x, z, 1 - c)

    def remote(src, dst, s, r, dev):
        return pltpu.make_async_remote_copy(
            src_ref=src, dst_ref=dst, send_sem=s, recv_sem=r, device_id=dev, device_id_type=MESH
        )

    pairs = [(k_in, k), (v_in, v), (tk_in, tk), (tv_in, tv), (q_in, q), (tq_in, tq), (go_in, go), (gain_in, gain)]
    loads = [pltpu.make_async_copy(s, d, in_sem.at[i]) for i, (s, d) in enumerate(pairs)]
    for load in loads:
        load.start()
    prior_loads = [
        pltpu.make_async_copy(
            prior_in.at[pl.ds(aligned(mine + p * PR + z * R, R), R)], prior.at[p], in_sem.at[len(pairs) + p]
        )
        for p in range(NP)
    ]
    for load in prior_loads:
        load.start()

    barrier = pltpu.get_barrier_semaphore()
    pl.semaphore_signal(barrier, inc=1, device_id=sibling, device_id_type=MESH)

    @pl.loop(1, Z)
    def _(n):
        pl.semaphore_signal(barrier, inc=1, device_id=seq_dev(x, lax.rem(z + n, Z), c), device_id_type=MESH)

    @pl.loop(1, X)
    def _(n):
        pl.semaphore_signal(barrier, inc=1, device_id=seq_dev(lax.rem(x + n, X), z, c), device_id_type=MESH)

    for n in range(1, Y):
        pl.semaphore_signal(barrier, inc=1, device_id={"head": lax.rem(y + n, Y)}, device_id_type=MESH)

    def core_copy(i, p):
        if p < NP:
            part = pl.ds(aligned(other + p * PR, PR), PR)
        else:
            part = pl.ds(aligned(mine, half * DH), half * DH)
        return remote(val.at[i, part], valx.at[i, part], core_s.at[i, p], core_r.at[i, p], sibling)

    def up_copy(i, p, zt, slot):
        src = chip.at[i, pl.ds(aligned(p * PR + zt * R, R), R)]
        return remote(src, up_rx.at[i, p, slot], up_s.at[i, p, zt], up_r.at[i, p, slot], seq_dev(x, zt, c))

    def x_copy(i, p, xt, slot):
        return remote(
            x_rx.at[i, p, x], x_rx.at[i, p, slot], x_s.at[i, p, xt], x_r.at[i, p, slot], seq_dev(xt, z, c)
        )

    def dn_copy(i, p, zt, slot):
        dst = full.at[i, pl.ds(aligned(mine + p * PR + slot * R, R), R)]
        return remote(dn_tx.at[i, p, zt], dst, dn_s.at[i, p, zt], dn_r.at[i, p, slot], seq_dev(x, zt, c))

    def rel_copy(i, p):
        part = pl.ds(aligned(mine + p * PR, PR), PR)
        return remote(full.at[i, part], full.at[i, part], rel_s.at[i, p], rel_r.at[i, p], sibling)

    def g_copy(p, zt, slot):
        return remote(g_tx.at[p], g_all.at[c, p, x, slot], g_s.at[p, zt], g_r.at[p, slot], seq_dev(x, zt, c))

    def gx_copy(p, xt, slot):
        return remote(
            g_all.at[c, p, x], g_all.at[c, p, slot], gx_s.at[p, xt], gx_r.at[p, slot], seq_dev(xt, z, c)
        )

    def gr_copy():
        return remote(g_all.at[c], g_all.at[c], gr_s.at[0], gr_r.at[0], sibling)

    def each_z(body):
        @pl.loop(0, Z - 1)
        def _(j):
            n = lax.rem(j + Z // 2 - 1, Z - 1) + 1
            body(lax.rem(z + n, Z))

    def each_x(body):
        @pl.loop(1, X)
        def _(n):
            body(lax.rem(x + n, X))

    def send_core(i, p):
        core_copy(i, p).start()

    def send_up(i, p):
        core_copy(i, p).wait_recv()
        part = pl.ds(aligned(mine + p * PR, PR), PR)
        chip[i, p * PR : (p + 1) * PR] = val[i, part] + valx[i, part]
        each_z(lambda zt: up_copy(i, p, zt, z).start())
        up_rx[i, p, z] = chip[i, pl.ds(aligned(p * PR + z * R, R), R)]

    def send_x(i, p):
        each_z(lambda zs: up_copy(i, p, zs, zs).wait_recv())
        total = up_rx[i, p, 0]
        for n in range(1, Z):
            total = total + up_rx[i, p, n]
        x_rx[i, p, x] = total
        each_x(lambda xt: x_copy(i, p, xt, x).start())

    def arrive_x(i, p):
        each_x(lambda xs: x_copy(i, p, xs, xs).wait_recv())

    def send_down(i, p):
        run = prior[p] if i == KV else jnp.zeros((R, DH), f32)
        for n in range(X):
            reached = (x < n) if i == QDO else (x > n)
            run = run + jnp.where(reached, x_rx[i, p, n], 0.0)
        for n in range(Z - 1, -1, -1) if i == QDO else range(Z):
            dn_tx[i, p, n] = run
            run = run + up_rx[i, p, n]
        each_z(lambda zt: dn_copy(i, p, zt, z).start())
        full[i, pl.ds(aligned(mine + p * PR + z * R, R), R)] = dn_tx[i, p, z]

    def send_total(p):
        piece = pl.ds(aligned(x * RX, RX), RX)
        total = x_rx[QDO, p, 0, piece]
        for n in range(1, X):
            total = total + x_rx[QDO, p, n, piece]
        g_tx[p] = total
        each_z(lambda zt: g_copy(p, zt, z).start())
        g_all[c, p, x, z] = total

    def spread_total(p):
        each_z(lambda zs: g_copy(p, zs, zs).wait_recv())
        each_x(lambda xt: gx_copy(p, xt, x).start())

    def relay(i, p):
        each_z(lambda zs: dn_copy(i, p, zs, zs).wait_recv())
        rel_copy(i, p).start()

    def finish(i):
        core_copy(i, NP).wait_recv()
        for p in range(NP):
            rel_copy(i, p).wait_recv()

    def entering(i, h):
        part = slice(h * DH, (h + 1) * DH)
        own_chip = (c == 0) if i == QDO else (c == 1)
        return (full[i, part] + jnp.where(own_chip, valx[i, part], 0.0)).astype(bf16)

    def cols(h):
        return pl.ds(aligned(h * DH, DH), DH)

    def head_rows(h):
        return pl.ds(aligned(h * DH, DH), DH)

    def key_value(h):
        val[KV, head_rows(h)] = tn(k[:, cols(h)], v[:, cols(h)])

    def tangent_key_value(h):
        val[TKV, head_rows(h)] = tn(tk[:, cols(h)], v[:, cols(h)]) + tn(k[:, cols(h)], tv[:, cols(h)])

    def over(first, count, body):
        for j in range(count):
            body(first + j)

    up_mask = lax.broadcasted_iota(jnp.int32, (rows, rows), 0) <= lax.broadcasted_iota(jnp.int32, (rows, rows), 1)
    low_mask = lax.broadcasted_iota(jnp.int32, (rows, rows), 0) >= lax.broadcasted_iota(jnp.int32, (rows, rows), 1)

    def masked(scores, mask):
        return jnp.where(mask, scores, 0.0).astype(bf16)

    def block_forward(lo, hi):
        @pl.loop(lo, hi)
        def _(h):
            qh, kh, vh = q[:, cols(h)], k[:, cols(h)], v[:, cols(h)]
            tqh, tkh, tvh = tq[:, cols(h)], tk[:, cols(h)], tv[:, cols(h)]
            a = masked(nt(qh, kh), low_mask)
            ta = masked(nt(tqh, kh) + nt(qh, tkh), low_mask)
            at[h] = masked(nt(kh, qh), up_mask)
            o[:, cols(h)] = nn(a, vh)
            to[:, cols(h)] = nn(ta, vh) + nn(a, tvh)

    def block_backward(lo, hi):
        @pl.loop(lo, hi)
        def _(h):
            qh, kh, vh, doh = q[:, cols(h)], k[:, cols(h)], v[:, cols(h)], do[:, cols(h)]
            da = masked(nt(doh, vh), low_mask)
            dat = masked(nt(vh, doh), up_mask)
            dq_out[:, cols(h)] = (nn(da, kh) + nt(doh, state[head_rows(h)])).astype(bf16)
            dkl[:, cols(h)] = nn(dat, qh)
            dvl[:, cols(h)] = nn(at[h], doh)

    def lane_sums(acc):
        return jnp.sum(acc[...].T, axis=0, keepdims=True)

    def spread(row):
        return jnp.broadcast_to(row, (DH, rows)).T

    def st_copy(i, yt, slot):
        return remote(st.at[i, y], st.at[i, slot], st_s.at[i, yt], st_r.at[i, slot], {"head": yt})

    def exchange(i, accs):
        st[i, y] = jnp.concatenate([lane_sums(a) for a in accs] + [jnp.zeros((8 - len(accs), rows), f32)], axis=0)
        for n in range(1, Y):
            st_copy(i, lax.rem(y + n, Y), y).start()

    def exchanged(i):
        for n in range(1, Y):
            ys = lax.rem(y + n, Y)
            st_copy(i, ys, ys).wait_recv()
        total = st[i, 0]
        for n in range(1, Y):
            total = total + st[i, n]
        return total

    outs = [(dq_out, dq_hbm), (dk_out, dk_hbm), (dv_out, dv_hbm), (tan_out, tan_hbm), (gs_out, gs_hbm)]
    stores = [pltpu.make_async_copy(s, d, out_sem.at[i]) for i, (s, d) in enumerate(outs)]

    def store_out(i):
        stores[i].start()

    loads[0].wait()
    loads[1].wait()
    over((1 - c) * half, half, key_value)
    pl.semaphore_wait(barrier, (C - 1) + (Z - 1) + (X - 1) + (Y - 1))
    for p in range(NP):
        send_core(KV, p)
    over(c * half, half, key_value)
    send_core(KV, NP)
    loads[2].wait()
    loads[3].wait()
    over((1 - c) * half, half, tangent_key_value)
    for p in range(NP):
        send_up(KV, p)
    for p in range(NP):
        send_core(TKV, p)
    over(c * half, half, tangent_key_value)
    send_core(TKV, NP)
    for p in range(NP):
        send_up(TKV, p)
    for load in loads[4:]:
        load.wait()
    for load in prior_loads:
        load.wait()
    block_forward(0, 3)
    send_x(KV, 0)
    send_x(KV, 1)
    block_forward(3, 5)
    for p in range(NP):
        arrive_x(KV, p)
        send_down(KV, p)
    send_x(TKV, 0)
    send_x(TKV, 1)
    block_forward(5, heads)
    relay(KV, 0)
    relay(KV, 1)
    for p in range(NP):
        arrive_x(TKV, p)
        send_down(TKV, p)
    finish(KV)
    acc_a[...] = jnp.zeros((rows, DH), f32)
    acc_b[...] = jnp.zeros((rows, DH), f32)
    for h in range(heads):
        part = slice(h * DH, (h + 1) * DH)
        state[part] = entering(KV, h)
        out = o[:, part] + nn(q[:, part], state[part])
        o[:, part] = out
        acc_a[...] += out * out
        acc_b[...] += out * (gain[h : h + 1] * go[:, part].astype(f32))
    exchange(0, [acc_a, acc_b])

    sums = exchanged(0)
    inv = 1.0 / jnp.sqrt(sums[0:1] / feats + eps)
    inv2 = inv * inv
    nrm[...] = spread(inv)
    back = spread(sums[1:2] / feats * inv * inv2)

    def cotangent(h):
        g = gain[pl.ds(h, 1)] * go[:, cols(h)].astype(f32)
        doh = (g * nrm[...] - o[:, cols(h)] * back).astype(bf16)
        do[:, cols(h)] = doh
        val[QDO, head_rows(h)] = tn(q[:, cols(h)], doh)

    over((1 - c) * half, half, cotangent)
    for p in range(NP):
        send_core(QDO, p)
    over(c * half, half, cotangent)
    send_core(QDO, NP)
    block_backward(0, 2)
    for p in range(NP):
        send_up(QDO, p)
    relay(TKV, 0)
    relay(TKV, 1)
    block_backward(2, 4)
    finish(TKV)
    acc_a[...] = jnp.zeros((rows, DH), f32)
    for h in range(heads):
        part = slice(h * DH, (h + 1) * DH)
        tout = to[:, part] + nn(tq[:, part], state[part]) + nn(q[:, part], entering(TKV, h))
        to[:, part] = tout
        acc_a[...] += o[:, part] * tout
    exchange(1, [acc_a])
    block_backward(4, 5)
    send_x(QDO, 0)
    send_x(QDO, 1)
    block_backward(5, heads)
    store_out(0)
    for p in range(NP):
        arrive_x(QDO, p)
        send_total(p)
    for p in range(NP):
        send_down(QDO, p)
    tangent = spread(exchanged(1)[0:1] / feats * inv * inv2)
    for h in range(heads):
        part = slice(h * DH, (h + 1) * DH)
        tan_out[:, part] = (gain[h : h + 1] * (to[:, part] * nrm[...] - o[:, part] * tangent)).astype(bf16)
    store_out(3)
    for p in range(NP):
        spread_total(p)
    relay(QDO, 0)
    relay(QDO, 1)
    for p in range(NP):
        each_x(lambda xs: gx_copy(p, xs, xs).wait_recv())
    gr_copy().start()
    finish(QDO)
    for h in range(heads):
        part = slice(h * DH, (h + 1) * DH)
        after = entering(QDO, h)
        dk_out[:, part] = (dkl[:, part] + nt(v[:, part], after)).astype(bf16)
        dv_out[:, part] = (dvl[:, part] + nn(k[:, part], after)).astype(bf16)
    store_out(1)
    store_out(2)
    gr_copy().wait_recv()
    for ch in range(C):
        for p in range(NP):
            for zs in range(Z):
                for xs in range(X):
                    at_ = ch * half * DH + p * PR + zs * R + xs * RX
                    gs_out[at_ : at_ + RX] = g_all[ch, p, xs, zs]
    store_out(4)
    for store in stores:
        store.wait()

    for i in range(3):
        for p in range(NP + 1):
            core_copy(i, p).wait_send()
        for p in range(NP):
            each_z(lambda zt: up_copy(i, p, zt, z).wait_send())
            each_x(lambda xt: x_copy(i, p, xt, x).wait_send())
            each_z(lambda zt: dn_copy(i, p, zt, z).wait_send())
            rel_copy(i, p).wait_send()
    for p in range(NP):
        each_z(lambda zt: g_copy(p, zt, z).wait_send())
        each_x(lambda xt: gx_copy(p, xt, x).wait_send())
    gr_copy().wait_send()
    for i in range(2):
        for n in range(1, Y):
            st_copy(i, lax.rem(y + n, Y), y).wait_send()


def copy_out(*refs):
    n = (len(refs) - 2) // 3
    ins, outs, held, in_sem, out_sem = refs[:n], refs[n : 2 * n], refs[2 * n : 3 * n], refs[-2], refs[-1]
    loads = [pltpu.make_async_copy(ins[i], held[i], in_sem.at[i]) for i in range(n)]
    stores = [pltpu.make_async_copy(held[i], outs[i], out_sem.at[i]) for i in range(n)]
    for load in loads:
        load.start()
    for load, store in zip(loads, stores):
        load.wait()
        store.start()
    for store in stores:
        store.wait()


def solution(mesh):
    X = mesh.shape["seq"] // (Z * C)
    Y = mesh.shape["head"]

    def per_device(query, key, value, grad_out, tan_query, tan_key, tan_value, norm_gain, prior_state):
        rows, width = query.shape
        heads = width // DH
        half = heads // C
        PR = half * DH // NP
        R = PR // Z
        vmem = pltpu.VMEM
        dma = pltpu.SemaphoreType.DMA
        wide = jax.ShapeDtypeStruct((rows, width), bf16)
        any_spec = pl.BlockSpec(memory_space=pl.ANY)
        outs = pl.pallas_call(
            functools.partial(kernel, X, Y, width * Y),
            out_shape=[wide] * 4 + [jax.ShapeDtypeStruct((heads * DH, DH), f32)],
            in_specs=[any_spec] * 9,
            out_specs=[any_spec] * 5,
            scratch_shapes=[vmem((rows, width), bf16)] * 4
            + [vmem((heads * DH, DH), f32), dma((5,))]
            + [vmem((rows, width), bf16)] * 7
            + [
                vmem((heads, DH), f32),
                vmem((NP, R, DH), f32),
                dma((8 + NP,)),
                vmem((3, heads * DH, DH), f32),
                vmem((3, heads * DH, DH), f32),
                vmem((3, half * DH, DH), f32),
                vmem((3, NP, Z, R, DH), f32),
                vmem((3, NP, X, R, DH), f32),
                vmem((3, NP, Z, R, DH), f32),
                vmem((3, heads * DH, DH), f32),
                vmem((NP, R // X, DH), f32),
                vmem((C, NP, X, Z, R // X, DH), f32),
                dma((3, NP + 1)),
                dma((3, NP + 1)),
                dma((3, NP, Z)),
                dma((3, NP, Z)),
                dma((3, NP, X)),
                dma((3, NP, X)),
                dma((3, NP, Z)),
                dma((3, NP, Z)),
                dma((3, NP)),
                dma((3, NP)),
                dma((NP, Z)),
                dma((NP, Z)),
                dma((NP, X)),
                dma((NP, X)),
                dma((1,)),
                dma((1,)),
                vmem((2, Y, 8, rows), f32),
                dma((2, Y)),
                dma((2, Y)),
                vmem((heads, rows, rows), bf16),
                vmem((rows, width), f32),
                vmem((rows, width), f32),
                vmem((rows, width), f32),
                vmem((rows, width), f32),
                vmem((rows, width), bf16),
                vmem((heads * DH, DH), bf16),
                vmem((heads * DH, DH), bf16),
                vmem((heads * DH, DH), bf16),
                vmem((rows, DH), f32),
                vmem((rows, DH), f32),
                vmem((rows, DH), f32),
            ],
            compiler_params=pltpu.CompilerParams(
                collective_id=0, has_side_effects=True, vmem_limit_bytes=60 * 1024 * 1024
            ),
        )(
            query, key, value, grad_out, tan_query, tan_key, tan_value,
            norm_gain.reshape(heads, DH), prior_state.reshape(heads * DH, DH),
        )
        outs = pl.pallas_call(
            copy_out,
            out_shape=[wide] * 4 + [jax.ShapeDtypeStruct((heads * DH, DH), f32)],
            in_specs=[any_spec] * 5,
            out_specs=[any_spec] * 5,
            scratch_shapes=[vmem((rows, width), bf16)] * 4 + [vmem((heads * DH, DH), f32), dma((5,)), dma((5,))],
        )(*outs)
        return (*outs[:4], outs[4].reshape(heads, DH, DH))

    wide, per_head = P("seq", "head"), P("head", None, None)
    return jax.shard_map(
        per_device,
        mesh=mesh,
        in_specs=(wide,) * 7 + (P("head"), per_head),
        out_specs=(wide,) * 4 + (per_head,),
        check_vma=False,
    )
```
